256 devices in a mesh: dom: 256 (over y, x, z, core).
Axes of the slice: x: 4, y: 4, z: 8, core: 2. Of those that a mesh axis runs over, the one named last changes fastest.
Arguments:
- embeddings: float32 [131072, 400], P('dom'), may hold values from -1.8 to 1.8
- row_state: float32 [131072], P('dom'), may hold values from 0.01 to 1
- relations: float32 [2048, 400], P('dom'), may hold values from 0.5 to 1.5
- relation_state: float32 [2048], P('dom'), may hold values from 0.01 to 1
- partner_mask: int32 [1], replicated, may hold values from 1 to 255
- source_rows: int32 [786432], P('dom'), may hold values from 0 to 511
- relation_ids: int32 [786432], P('dom'), may hold values from 0 to 2047
- dest_rows: int32 [786432], P('dom'), may hold values from 0 to 511
- negative_rows: int32 [3072, 512], P('dom'), may hold values from 0 to 511
- edge_count: int32 [256], P('dom'), may hold values from 1 to 3072, 491520 in all
Outputs:
- new_embeddings: float32 [131072, 400], P('dom')
- new_row_state: float32 [131072], P('dom')
- new_relations: float32 [2048, 400], P('dom')
- new_relation_state: float32 [2048], P('dom')
The draws below stay inside these ranges and needn't reach their ends.
Inputs may be any that keep to these rules, and one draw needn't show every extreme that they name: Device i trains the bucket of partition i with partition i XOR partner_mask[0]. `edge_count`: some bucket has all 3072 slots live.
All inputs are finite; a program needn't handle non-finite values. No bound on the sum of `edge_count` on one device may be relied on, other than what follows from the above.
Results may differ from the reference program's by a relative error of at most 0.0015.
Values may be sent and summed in bfloat16 or wider, within the bound.
No kernel may reach another device: no remote copies, remote signals or barrier semaphores. Data moves between devices by JAX's collectives and lax.ppermute only.
A program may use at most 128 MiB of HBM per device.

```python
import math
import jax
import jax.numpy as jnp
import numpy as np
from jax import lax

D = 400
RELS = 2048
ROWS = 512
EDGES = 3072
NEGS = 512
GROUPS = 12
ALL_ROWS = 131072
ALL_EDGES = 786432
ALL_GROUPS = 3072
N_DOM = 256


def touch_ends(array, rng, low, largest):
    shape = array.shape
    index_at = [jax.random.randint(jax.random.fold_in(rng, axis), (), 0, shape[axis]) for axis in range(len(shape))]
    array = array.at[tuple(index_at)].set(low)
    longest = shape.index(max(shape))
    index_at[longest] = (index_at[longest] + 1) % shape[longest]
    return array.at[tuple(index_at)].set(largest)


def block_scale(key, dims, shards, smallest, largest):
    level = 1.0
    for axis_at, blocks in shards:
        steps = jax.random.uniform(jax.random.fold_in(jax.random.fold_in(key, 6), axis_at), (blocks,), jnp.float32, smallest / len(shards), largest / len(shards))
        level = level * jnp.repeat(jnp.exp(steps), dims[axis_at] // blocks).reshape((-1,) + (1,) * (len(dims) - 1 - axis_at))
    return level


def rank_table(amount, skew):
    loads = [(1 << 20) // math.isqrt(grade ** skew) + 1 for grade in range(1, amount + 1)]
    scale = 1 + sum(loads) // (1 << 30)
    return np.cumsum(np.array([max(1, weight // scale) for weight in loads]))


def ranked(stream_key, extent, number_of, slope):
    listing = rank_table(number_of, slope)
    ticket = jax.random.randint(jax.random.fold_in(stream_key, 1), extent, 0, int(listing[number_of - 1]))
    rank = jnp.searchsorted(jnp.asarray(listing, jnp.int32), ticket, side="right")
    return jax.random.permutation(jax.random.fold_in(stream_key, 2), number_of)[rank].astype(jnp.int32)


def length_profile(number_of, total, reach, skew):
    loads = [(1 << 20) // math.isqrt(rank ** skew) + 1 for rank in range(2, number_of + 1)]
    rest, given = total - reach - (number_of - 1), [1] * (number_of - 1)
    while rest > 0:
        free = [i for i in range(number_of - 1) if given[i] < reach]
        pool, budget = sum([loads[i] for i in free]), rest
        for i in free:
            addition = min(reach - given[i], max(1, budget * loads[i] // pool), rest)
            given[i] = given[i] + addition
            rest = rest - addition
    return np.array([reach] + given)


def ragged(stream_key, count, total, bound, lean):
    if count == 2:
        one = jax.random.randint(stream_key, (), max(1, total - bound), min(bound, total - 1) + 1)
        return jnp.stack([one, total - one])
    lengths = jnp.asarray(length_profile(count, total, bound, lean), jnp.int32)
    twos = (count - 1) // 2
    giver, receiver = lengths[1:1 + 2 * twos:2], lengths[2:2 + 2 * twos:2]
    slack = jnp.minimum(giver - 1, bound - receiver)
    moved = jax.random.randint(jax.random.fold_in(stream_key, 1), (twos,), 0, 1 << 20) % (slack + 1)
    lengths = lengths.at[1:1 + 2 * twos:2].set(giver - moved).at[2:2 + 2 * twos:2].set(receiver + moved)
    return lengths[jax.random.permutation(jax.random.fold_in(stream_key, 2), count)]


def gaussian(key, dims, deviation, limit, pieces=(), kind=jnp.bfloat16):
    factor_of = block_scale(key, dims, pieces, -0.22, 0.18) if pieces else 1.0
    result = jax.random.normal(key, dims, jnp.float32) * deviation * factor_of
    return jnp.minimum(jnp.maximum(result, -limit), limit).astype(kind)


def setup_inputs(seed: int = 0) -> dict:
    key_list = jax.random.split(jax.random.key(seed), 11)
    return {
        "embeddings": gaussian(key_list[0], (ALL_ROWS, D), 0.3, 1.8, ((0, 256),), jnp.float32),
        "row_state": jnp.clip(jnp.exp(math.log(1.0) - 4.6051702 * jax.random.uniform(key_list[1], (ALL_ROWS,), jnp.float32) ** block_scale(key_list[1], (ALL_ROWS,), ((0, 256),), -0.2, 0.2)), 0.01, 1.0),
        "relations": jnp.clip(1.0 + 0.1 * jax.random.normal(key_list[2], (RELS, D), jnp.float32), 0.5, 1.5),
        "relation_state": jnp.clip(jnp.exp(math.log(1.0) - 4.6051702 * jax.random.uniform(key_list[3], (RELS,), jnp.float32) ** block_scale(key_list[3], (RELS,), ((0, 256),), -0.2, 0.2)), 0.01, 1.0),
        "partner_mask": jax.random.randint(key_list[4], (1,), 1, N_DOM).astype(jnp.int32),
        "source_rows": touch_ends(jax.random.randint(key_list[5], (ALL_EDGES,), 0, ROWS), jax.random.fold_in(key_list[5], 1), 0, ROWS - 1).astype(jnp.int32),
        "relation_ids": touch_ends(ranked(key_list[6], (ALL_EDGES,), RELS, 1), jax.random.fold_in(key_list[6], 3), 0, RELS - 1).astype(jnp.int32),
        "dest_rows": touch_ends(jax.random.randint(key_list[7], (ALL_EDGES,), 0, ROWS), jax.random.fold_in(key_list[7], 1), 0, ROWS - 1).astype(jnp.int32),
        "negative_rows": touch_ends(jax.random.randint(key_list[8], (ALL_GROUPS, NEGS), 0, ROWS), jax.random.fold_in(key_list[8], 1), 0, ROWS - 1).astype(jnp.int32),
        "edge_count": ragged(key_list[9], N_DOM, EDGES * N_DOM * 5 // 8, EDGES, 2).astype(jnp.int32),
    }


def train_bucket(own_bf, part_bf, rel_bf, source, rel_ids, target_rows, negatives, live_count):
    groups, negs_per = negatives.shape
    edges = source.shape[0]
    group_len = edges // groups
    width = own_bf.shape[1]
    own_rows = own_bf[source].astype(jnp.float32)
    rel_rows = rel_bf[rel_ids].astype(jnp.float32)
    queries = (own_rows * rel_rows).astype(jnp.bfloat16)
    query_full = queries.astype(jnp.float32)
    targets = part_bf[target_rows].astype(jnp.float32)
    positive = lax.optimization_barrier(jnp.sum(query_full * targets, axis=1))
    sampled = part_bf[negatives].astype(jnp.float32)
    grouped = query_full.reshape(groups, group_len, width)
    scores = jnp.einsum('gkd,gnd->gkn', grouped, sampled)
    live = (jnp.arange(edges, dtype=jnp.int32) < live_count).astype(jnp.float32)
    pos_grad = -live * jax.nn.sigmoid(-positive)
    neg_grad = (live.reshape(groups, group_len, 1) * jax.nn.sigmoid(scores) / negs_per).astype(jnp.bfloat16)
    neg_full = neg_grad.astype(jnp.float32)
    query_grad = pos_grad[:, None] * targets + jnp.einsum('gkn,gnd->gkd', neg_full, sampled).reshape(edges, width)
    own_grad = jnp.zeros((own_bf.shape[0], width), jnp.float32).at[source].add(query_grad * rel_rows)
    rel_grad = jnp.zeros((rel_bf.shape[0], width), jnp.float32).at[rel_ids].add(query_grad * own_rows)
    neg_terms = jnp.einsum('gkn,gkd->gnd', neg_full, grouped).reshape(groups * negs_per, width)
    part_grad = jnp.zeros((part_bf.shape[0], width), jnp.float32).at[target_rows].add(pos_grad[:, None] * query_full)
    part_grad = part_grad.at[negatives.reshape(-1)].add(neg_terms)
    return (own_grad, part_grad.astype(jnp.bfloat16), rel_grad)

def reference(embeddings, row_state, relations, relation_state, partner_mask, source_rows, relation_ids, dest_rows, negative_rows, edge_count):
    blocks = embeddings.astype(jnp.bfloat16).reshape(N_DOM, ROWS, D)
    rel_bf = relations.astype(jnp.bfloat16)
    partner = jnp.bitwise_xor(jnp.arange(N_DOM, dtype=jnp.int32), partner_mask[0])
    sources = source_rows.reshape(N_DOM, EDGES)
    rel_all = relation_ids.reshape(N_DOM, EDGES)
    targets = dest_rows.reshape(N_DOM, EDGES)
    negatives = negative_rows.reshape(N_DOM, GROUPS, NEGS)

    def visit(summed, device):
        own_grad, part_grad, rel_grad = train_bucket(blocks[device], blocks[partner[device]], rel_bf, sources[device], rel_all[device], targets[device], negatives[device], edge_count[device])
        return (summed + rel_grad, (own_grad, part_grad))
    rel_total, (own_grads, part_grads) = lax.scan(visit, jnp.zeros((RELS, D), jnp.float32), jnp.arange(N_DOM, dtype=jnp.int32))
    grad = (own_grads + part_grads[partner].astype(jnp.float32)).reshape(ALL_ROWS, D)
    new_row_state = row_state + lax.optimization_barrier(jnp.mean(grad * grad, axis=1))
    new_embeddings = embeddings - 0.1 * grad / jnp.sqrt(new_row_state)[:, None]
    new_relation_state = relation_state + lax.optimization_barrier(jnp.mean(rel_total * rel_total, axis=1))
    new_relations = relations - 0.1 * rel_total / jnp.sqrt(new_relation_state)[:, None]
    return (new_embeddings, new_row_state, new_relations, new_relation_state)
```

```python
import jax
import jax.numpy as jnp
from jax import lax
from jax.experimental import pallas as pl
from jax.experimental.pallas import tpu as pltpu
from jax.sharding import PartitionSpec as P

BF = jnp.bfloat16
F32 = jnp.float32
NT = (((1,), (1,)), ((), ()))
NN = (((1,), (0,)), ((), ()))

CORE_BITS, Z_BITS, XY_BITS = 1, 3, 4
Z_SHIFT, XY_SHIFT = CORE_BITS, CORE_BITS + Z_BITS


def dot(a, b, dims):
    return lax.dot_general(a, b, dims, preferred_element_type=F32)


def one_hot(rows, ids, base=0):
    iota = lax.broadcasted_iota(jnp.int32, (rows, ids.shape[1]), 0)
    return iota == (ids - base)


def train_kernel(cnt_ref, bt_ref, pt_ref, r0_ref, r1_ref, s_ref, r_ref, d_ref, n_ref, rall_ref,
                 own_ref, part_ref, g0_ref, g1_ref,
                 rt, p, qa, wa, xo, xr, oa):
    width, rows = pt_ref.shape
    groups, glen = s_ref.shape
    half = r0_ref.shape[0]
    rels = 2 * half
    negs = n_ref.shape[1]
    ident = (lax.broadcasted_iota(jnp.int32, (width, width), 0)
             == lax.broadcasted_iota(jnp.int32, (width, width), 1)).astype(BF)
    rt[:, :half] = dot(ident, r0_ref[...], NT).astype(BF)
    rt[:, half:] = dot(ident, r1_ref[...], NT).astype(BF)
    ident_r = (lax.broadcasted_iota(jnp.int32, (rows, rows), 0)
               == lax.broadcasted_iota(jnp.int32, (rows, rows), 1)).astype(BF)
    p[...] = dot(ident_r, pt_ref[...], NT).astype(BF)
    live_count = cnt_ref[0]
    ones = jnp.ones((negs, glen), BF)

    def group(g, carry):
        at = pl.ds(pl.multiple_of(g * glen, glen), glen)
        sel_s = one_hot(rows, s_ref[pl.ds(g, 1), :]).astype(BF)
        oa[:, at] = sel_s
        own = dot(bt_ref[...], sel_s, NN)
        rel = dot(rt[...], one_hot(rels, r_ref[pl.ds(g, 1), :]).astype(BF), NN)
        query = (own * rel).astype(BF)
        qa[:, at] = query
        score = dot(p[...], query, NN)
        hit = one_hot(rows, d_ref[pl.ds(g, 1), :])
        positive = jnp.sum(jnp.where(hit, score, 0.0), axis=0, keepdims=True)
        edge = g * glen + lax.broadcasted_iota(jnp.int32, (1, glen), 1)
        live = jnp.where(edge < live_count, 1.0, 0.0)
        pos_grad = -live * (0.5 - 0.5 * jnp.tanh(0.5 * positive))
        times = dot(one_hot(rows, n_ref[pl.ds(g, 1), :]).astype(BF), ones, NN)
        neg = (live * (0.5 / negs) * (jnp.tanh(0.5 * score) + 1.0)).astype(BF).astype(F32)
        weight = times * neg
        weight = jnp.where(hit, weight + pos_grad, weight).astype(BF)
        wa[:, at] = weight
        grad = dot(pt_ref[...], weight, NN)
        xo[:, at] = (grad * rel).astype(BF)
        xr[:, at] = (grad * own).astype(BF)
        return carry

    lax.fori_loop(0, groups, group, 0)
    part_ref[...] = dot(qa[...], wa[...], NT).astype(BF)
    own_ref[...] = dot(xo[...], oa[...], NT)
    tile = 256
    for t in range(rels // tile):
        sel = one_hot(tile, rall_ref[...], t * tile).astype(BF)
        out = dot(sel, xr[...], NT).astype(BF)
        g_ref, base = (g0_ref, t * tile) if t * tile < half else (g1_ref, t * tile - half)
        g_ref[base:base + tile, :] = out


def train(cnt, bt, pt, r0, r1, s, r, d, n):
    width, rows = pt.shape
    half = r0.shape[0]
    edges = s.size
    vm = pl.BlockSpec(memory_space=pltpu.VMEM)
    return pl.pallas_call(
        train_kernel,
        out_shape=(jax.ShapeDtypeStruct((width, rows), F32), jax.ShapeDtypeStruct((width, rows), BF),
                   jax.ShapeDtypeStruct((half, width), BF), jax.ShapeDtypeStruct((half, width), BF)),
        in_specs=[pl.BlockSpec(memory_space=pltpu.SMEM)] + [vm] * 9,
        out_specs=(vm,) * 4,
        scratch_shapes=[pltpu.VMEM((width, 2 * half), BF), pltpu.VMEM((rows, width), BF),
                        pltpu.VMEM((width, edges), BF), pltpu.VMEM((rows, edges), BF),
                        pltpu.VMEM((width, edges), BF), pltpu.VMEM((width, edges), BF),
                        pltpu.VMEM((rows, edges), BF)],
        name="train",
    )(cnt, bt, pt, r0, r1, s, r, d, n, r.reshape(1, edges))


def swap(value, mask):
    pairs = [(source, source ^ mask) for source in range(lax.axis_size("dom"))]
    return lax.ppermute(value, "dom", pairs)


def groups_of(shift, bits):
    members = [m << shift for m in range(1 << bits)]
    rest = [b for b in range(lax.axis_size("dom")) if not b & (((1 << bits) - 1) << shift)]
    return [[b | m for m in members] for b in rest]


def exchange(blocks, shift, bits):
    return lax.all_to_all(blocks, "dom", 0, 0, axis_index_groups=groups_of(shift, bits))


def partner_step(mask, shift, bits, value, side, side_input):
    def branch(digit):
        def run(operands):
            moved, extra = operands
            if digit:
                moved = swap(moved, digit << shift)
            return moved, side(extra)

        return run

    digit = jnp.bitwise_and(jnp.right_shift(mask, shift), (1 << bits) - 1)
    return lax.switch(digit, [branch(m) for m in range(1 << bits)], (value, side_input))


def added(blocks):
    return jnp.sum(blocks.astype(F32), axis=0).astype(BF)


def local(
    embeddings,
    row_state,
    relations,
    relation_state,
    partner_mask,
    source_rows,
    relation_ids,
    dest_rows,
    negative_rows,
    edge_count,
):
    mask = partner_mask[0]
    groups = negative_rows.shape[0]
    rel_local, width = relations.shape
    me = lax.axis_index("dom")
    odd = jnp.bitwise_and(mask, 1) == 1
    z_size, xy_size = 1 << Z_BITS, 1 << XY_BITS
    half = z_size * xy_size * rel_local

    own_t = embeddings.astype(BF).T
    rel_bf = relations.astype(BF)

    def gather_z(block):
        blocks = jnp.broadcast_to(block[None], (z_size,) + block.shape)
        return exchange(blocks, Z_SHIFT, Z_BITS).reshape(z_size * block.shape[0], width)

    def gather_xy(block):
        blocks = jnp.broadcast_to(block[None], (xy_size,) + block.shape)
        return exchange(blocks, XY_SHIFT, XY_BITS).reshape(xy_size * block.shape[0], width)

    part_t, rel_z = partner_step(mask, XY_SHIFT, XY_BITS, own_t, gather_z, rel_bf)
    part_t, rel_here = partner_step(mask, Z_SHIFT, Z_BITS, part_t, gather_xy, rel_z)
    rel_there = swap(rel_here, 1)
    part_t = jnp.where(odd, swap(part_t, 1), part_t)

    owner = relation_ids // rel_local
    core = jnp.bitwise_and(jnp.bitwise_xor(owner, me), 1)
    spot = core * half + jnp.right_shift(owner, CORE_BITS) * rel_local + relation_ids % rel_local

    own_grad, part_grad, grad_here, grad_there = train(
        edge_count, own_t, part_t, rel_here, rel_there,
        source_rows.reshape(groups, -1), spot.reshape(groups, -1),
        dest_rows.reshape(groups, -1), negative_rows,
    )

    from_core = swap(grad_there, 1)
    part_core = swap(part_grad, 1)
    returned = jnp.where(odd, part_core, part_grad)
    grad_sum = (grad_here.astype(F32) + from_core.astype(F32)).astype(BF)

    def scatter_xy(table):
        return added(exchange(table.reshape(xy_size, z_size * rel_local, width), XY_SHIFT, XY_BITS))

    def scatter_z(table):
        return exchange(table.reshape(z_size, rel_local, width), Z_SHIFT, Z_BITS)

    returned, grad_xy = partner_step(mask, Z_SHIFT, Z_BITS, returned, scatter_xy, grad_sum)
    returned, grad_z = partner_step(mask, XY_SHIFT, XY_BITS, returned, scatter_z, grad_xy)

    grad = (own_grad + returned.astype(F32)).T
    new_row_state = row_state + jnp.mean(grad * grad, axis=1)
    new_embeddings = embeddings - 0.1 * grad / jnp.sqrt(new_row_state)[:, None]
    rel_total = jnp.sum(grad_z.astype(F32), axis=0)
    new_relation_state = relation_state + jnp.mean(rel_total * rel_total, axis=1)
    new_relations = relations - 0.1 * rel_total / jnp.sqrt(new_relation_state)[:, None]
    return (new_embeddings, new_row_state, new_relations, new_relation_state)


def solution(mesh):
    in_specs = (
        P("dom", None),
        P("dom"),
        P("dom", None),
        P("dom"),
        P(),
        P("dom"),
        P("dom"),
        P("dom"),
        P("dom", None),
        P("dom"),
    )
    out_specs = (P("dom", None), P("dom"), P("dom", None), P("dom"))
    return jax.shard_map(local, mesh=mesh, in_specs=in_specs, out_specs=out_specs, check_vma=False)
```

```python
import jax
import jax.numpy as jnp
from jax import lax
from jax.experimental import pallas as pl
from jax.experimental.pallas import tpu as pltpu
from jax.sharding import PartitionSpec as P

BF = jnp.bfloat16
F32 = jnp.float32
NT = (((1,), (1,)), ((), ()))
NN = (((1,), (0,)), ((), ()))

CORE_BITS, Z_BITS, XY_BITS = 1, 3, 4
Z_SHIFT, XY_SHIFT = CORE_BITS, CORE_BITS + Z_BITS


TILE = 256


def dot(a, b, dims):
    return lax.dot_general(a, b, dims, preferred_element_type=F32)


def one_hot(ids, tile):
    low = jnp.where(jnp.right_shift(ids, 8) == tile, jnp.bitwise_and(ids, TILE - 1), -1)
    low = jnp.broadcast_to(low.astype(F32), (TILE, ids.shape[1])).astype(BF)
    rows = lax.broadcasted_iota(jnp.int32, (TILE, ids.shape[1]), 0).astype(F32).astype(BF)
    return jnp.where(rows == low, jnp.ones((), BF), jnp.zeros((), BF))


def one_hots(ids, size):
    return jnp.concatenate([one_hot(ids, t) for t in range(size // TILE)], axis=0)


def identity(n):
    return (lax.broadcasted_iota(jnp.int32, (n, n), 0) == lax.broadcasted_iota(jnp.int32, (n, n), 1)).astype(BF)


def first_kernel(bt_ref, s_ref, n_ref, own_ref, sel_ref, times_ref):
    rows = bt_ref.shape[1]
    groups, glen = s_ref.shape
    negs = n_ref.shape[1]

    def group(g, carry):
        at = pl.ds(pl.multiple_of(g * glen, glen), glen)
        sel = one_hots(s_ref[pl.ds(g, 1), :], rows)
        sel_ref[:, at] = sel
        own_ref[:, at] = dot(bt_ref[...], sel, NN).astype(BF)
        hits = one_hots(n_ref[pl.ds(g, 1), :], rows)
        lanes = negs // 4
        four = (hits[:, :lanes] + hits[:, lanes:2 * lanes]) + (hits[:, 2 * lanes:3 * lanes] + hits[:, 3 * lanes:])
        times = jnp.sum(four.astype(F32), axis=1, keepdims=True) * (0.5 / negs)
        times_ref[pl.ds(g, 1)] = jnp.broadcast_to(times, (rows, 128)).astype(BF)[None]
        return carry

    lax.fori_loop(0, groups, group, 0)


def train_kernel(own_ref, times_ref, pt_ref, r0_ref, r1_ref, r_ref, d_ref, rall_ref,
                 part_ref, xo_ref, g0_ref, g1_ref,
                 rt, p, qa, wa, xr, sc0, rl0):
    width, rows = pt_ref.shape
    groups, glen = d_ref.shape
    half = r0_ref.shape[0]
    rels = 2 * half
    ident = identity(width)
    wide = 2 * TILE
    for k, ref in enumerate((r0_ref, r1_ref)):
        def turn(t, carry, k=k, ref=ref):
            at = pl.multiple_of(t * wide, wide)
            rt[:, pl.ds(k * half + at, wide)] = dot(ident, ref[pl.ds(at, wide), :], NT).astype(BF)
            return carry

        lax.fori_loop(0, half // wide, turn, 0)
    p[...] = (0.5 * dot(identity(rows), pt_ref[...], NT)).astype(BF)

    def span(g):
        return pl.ds(pl.multiple_of(g * glen, glen), glen)

    def forward(g, sc, rl):
        rel = dot(rt[...], one_hots(r_ref[pl.ds(g, 1), :], rels), NN).astype(BF)
        rl[...] = rel
        query = own_ref[:, span(g)] * rel
        qa[:, span(g)] = query
        sc[...] = dot(p[...], query, NN)

    def backward(g, sc, rl):
        score = sc[...]
        row = lax.broadcasted_iota(jnp.int32, (rows, glen), 0)
        hit = row == d_ref[pl.ds(g, 1), :]
        positive = jnp.sum(jnp.where(hit, score, 0.0), axis=0, keepdims=True)
        pos_grad = 0.5 * jnp.tanh(positive) - 0.5
        times = times_ref[pl.ds(g, 1)][0].astype(F32)
        times = jnp.concatenate([times, times], axis=1)
        weight = (jnp.tanh(score) + 1.0) * times
        weight = jnp.where(hit, weight + pos_grad, weight).astype(BF)
        wa[:, span(g)] = weight
        grad = dot(pt_ref[...], weight, NN).astype(BF)
        xo_ref[:, span(g)] = grad * rl[...]
        xr[:, span(g)] = grad * own_ref[:, span(g)]

    def group(g, carry):
        forward(g, sc0, rl0)
        backward(g, sc0, rl0)
        return carry

    lax.fori_loop(0, groups, group, 0)
    part_ref[...] = dot(qa[...], wa[...], NT).astype(BF)

    tiles = half // TILE

    def scatter(t, carry):
        out = dot(xr[...], one_hot(rall_ref[...], t), NT).T.astype(BF)
        at = pl.ds(pl.multiple_of(lax.rem(t, tiles) * TILE, TILE), TILE)

        @pl.when(t < tiles)
        def _():
            g0_ref[at, :] = out

        @pl.when(t >= tiles)
        def _():
            g1_ref[at, :] = out

        return carry

    lax.fori_loop(0, rels // TILE, scatter, 0)


def last_kernel(xo_ref, sel_ref, own_ref):
    own_ref[...] = dot(xo_ref[...], sel_ref[...], NT)


def swap(value, mask):
    pairs = [(source, source ^ mask) for source in range(lax.axis_size("dom"))]
    return lax.ppermute(value, "dom", pairs)


def groups_of(shift, bits):
    members = [m << shift for m in range(1 << bits)]
    rest = [b for b in range(lax.axis_size("dom")) if not b & (((1 << bits) - 1) << shift)]
    return [[b | m for m in members] for b in rest]


def exchange(blocks, shift, bits):
    return lax.all_to_all(blocks, "dom", 0, 0, axis_index_groups=groups_of(shift, bits))


def partner_step(mask, shift, bits, value):
    def branch(digit):
        return lambda moved: swap(moved, digit << shift) if digit else moved

    digit = jnp.bitwise_and(jnp.right_shift(mask, shift), (1 << bits) - 1)
    return lax.switch(digit, [branch(m) for m in range(1 << bits)], value)


def added(blocks):
    return jnp.sum(blocks.astype(F32), axis=0).astype(BF)


def local(
    embeddings,
    row_state,
    relations,
    relation_state,
    partner_mask,
    source_rows,
    relation_ids,
    dest_rows,
    negative_rows,
    edge_count,
):
    mask = partner_mask[0]
    groups = negative_rows.shape[0]
    rel_local, width = relations.shape
    rows = embeddings.shape[0]
    edges = source_rows.shape[0]
    me = lax.axis_index("dom")
    odd = jnp.bitwise_and(mask, 1) == 1
    z_size, xy_size = 1 << Z_BITS, 1 << XY_BITS
    half = z_size * xy_size * rel_local
    vm = pl.BlockSpec(memory_space=pltpu.VMEM)
    sh = jax.ShapeDtypeStruct

    own_t = embeddings.astype(BF).T
    rel_bf = relations.astype(BF)
    live = jnp.arange(edges, dtype=jnp.int32) < edge_count[0]
    own_edges, own_sel, times = pl.pallas_call(
        first_kernel,
        out_shape=(sh((width, edges), BF), sh((rows, edges), BF), sh((groups, rows, 128), BF)),
        in_specs=[vm] * 3, out_specs=(vm,) * 3, name="first",
    )(own_t, jnp.where(live, source_rows, -1).reshape(groups, -1), negative_rows)

    def spread(block, size):
        return jnp.broadcast_to(block[None], (size,) + block.shape)

    part_t = partner_step(mask, XY_SHIFT, XY_BITS, own_t)
    rel_z = exchange(spread(rel_bf, z_size), Z_SHIFT, Z_BITS).reshape(z_size * rel_local, width)
    rel_z, part_t = lax.optimization_barrier((rel_z, part_t))
    part_t = partner_step(mask, Z_SHIFT, Z_BITS, part_t)
    rel_here = exchange(spread(rel_z, xy_size), XY_SHIFT, XY_BITS)
    rel_here, part_t, own_edges = lax.optimization_barrier((rel_here, part_t, own_edges))
    rel_there = swap(rel_here, 1)
    part_t = jnp.where(odd, swap(part_t, 1), part_t)

    owner = relation_ids // rel_local
    core = jnp.bitwise_and(jnp.bitwise_xor(owner, me), 1)
    spot = core * half + jnp.right_shift(owner, CORE_BITS) * rel_local + relation_ids % rel_local

    part_grad, to_source, grad_here, grad_there = pl.pallas_call(
        train_kernel,
        out_shape=(sh((width, rows), BF), sh((width, edges), BF), sh((half, width), BF), sh((half, width), BF)),
        in_specs=[vm] * 8, out_specs=(vm,) * 4,
        scratch_shapes=[pltpu.VMEM((width, 2 * half), BF), pltpu.VMEM((rows, width), BF),
                        pltpu.VMEM((width, edges), BF), pltpu.VMEM((rows, edges), BF),
                        pltpu.VMEM((width, edges), BF),
                        pltpu.VMEM((rows, edges // groups), F32), pltpu.VMEM((width, edges // groups), BF)],
        name="train",
    )(own_edges, times, part_t, rel_here.reshape(half, width), rel_there.reshape(half, width),
      spot.reshape(groups, -1), dest_rows.reshape(groups, -1), spot.reshape(1, edges))

    by_z = (xy_size, z_size * rel_local, width)
    from_core = swap(grad_there.reshape(by_z), 1)
    part_core = swap(part_grad, 1)
    own_grad = pl.pallas_call(
        last_kernel, out_shape=sh((width, rows), F32), in_specs=[vm] * 2, out_specs=vm, name="last",
    )(to_source, own_sel)
    returned = jnp.where(odd, part_core, part_grad)
    grad_sum = (grad_here.reshape(by_z).astype(F32) + from_core.astype(F32)).astype(BF)
    grad_xy = added(exchange(grad_sum, XY_SHIFT, XY_BITS))
    returned = partner_step(mask, Z_SHIFT, Z_BITS, returned)
    grad_xy, returned, own_grad = lax.optimization_barrier((grad_xy, returned, own_grad))
    grad_z = exchange(grad_xy.reshape(z_size, rel_local, width), Z_SHIFT, Z_BITS)
    returned = partner_step(mask, XY_SHIFT, XY_BITS, returned)

    grad = (own_grad + returned.astype(F32)).T
    new_row_state = row_state + jnp.mean(grad * grad, axis=1)
    new_embeddings = embeddings - 0.1 * grad / jnp.sqrt(new_row_state)[:, None]
    rel_total = jnp.sum(grad_z.astype(F32), axis=0)
    new_relation_state = relation_state + jnp.mean(rel_total * rel_total, axis=1)
    new_relations = relations - 0.1 * rel_total / jnp.sqrt(new_relation_state)[:, None]
    return (new_embeddings, new_row_state, new_relations, new_relation_state)


def solution(mesh):
    in_specs = (
        P("dom", None),
        P("dom"),
        P("dom", None),
        P("dom"),
        P(),
        P("dom"),
        P("dom"),
        P("dom"),
        P("dom", None),
        P("dom"),
    )
    out_specs = (P("dom", None), P("dom"), P("dom", None), P("dom"))
    return jax.shard_map(local, mesh=mesh, in_specs=in_specs, out_specs=out_specs, check_vma=False)
```

```python
import jax
import jax.numpy as jnp
from jax import lax
from jax.experimental import pallas as pl
from jax.experimental.pallas import tpu as pltpu
from jax.sharding import PartitionSpec as P

BF = jnp.bfloat16
F32 = jnp.float32
NT = (((1,), (1,)), ((), ()))
NN = (((1,), (0,)), ((), ()))

CORE_BITS, Z_BITS, XY_BITS = 1, 3, 4
Z_SHIFT, XY_SHIFT = CORE_BITS, CORE_BITS + Z_BITS


TILE = 256


def dot(a, b, dims):
    return lax.dot_general(a, b, dims, preferred_element_type=F32)


def one_hot(ids, tile):
    low = jnp.where(jnp.right_shift(ids, 8) == tile, jnp.bitwise_and(ids, TILE - 1), -1)
    low = jnp.broadcast_to(low.astype(F32), (TILE, ids.shape[1])).astype(BF)
    rows = lax.broadcasted_iota(jnp.int32, (TILE, ids.shape[1]), 0).astype(F32).astype(BF)
    return jnp.where(rows == low, jnp.ones((), BF), jnp.zeros((), BF))


def one_hots(ids, size):
    return jnp.concatenate([one_hot(ids, t) for t in range(size // TILE)], axis=0)


def identity(n):
    return (lax.broadcasted_iota(jnp.int32, (n, n), 0) == lax.broadcasted_iota(jnp.int32, (n, n), 1)).astype(BF)


def train_kernel(odd_ref, bt_ref, pa_ref, pb_ref, r0_ref, r1_ref, s_ref, r_ref, d_ref, n_ref, rall_ref,
                 part_ref, xo_ref, g0_ref, g1_ref,
                 rt, pt, p, own, rl, qa, wa, xr, times_all, sc0, sc1):
    width, rows = pa_ref.shape
    groups, negs = n_ref.shape
    edges = rall_ref.shape[1]
    glen = edges // groups
    half = r0_ref.shape[0]
    rels = 2 * half
    ident = identity(width)
    wide = TILE
    pt[...] = jnp.where(odd_ref[0] == 1, pb_ref[...], pa_ref[...])
    p[...] = (0.5 * pt[...].astype(F32)).T.astype(BF)
    for k, ref in enumerate((r0_ref, r1_ref)):
        def turn(t, carry, k=k, ref=ref):
            at = pl.multiple_of(t * wide, wide)
            rt[:, pl.ds(k * half + at, wide)] = dot(ident, ref[pl.ds(at, wide), :], NT).astype(BF)
            return carry

        lax.fori_loop(0, half // wide, turn, 0)

    def span(g):
        return pl.ds(pl.multiple_of(g * glen, glen), glen)

    def ids(ref, g):
        lines = glen // 128
        got = ref[pl.ds(g * lines, lines), :]
        return jnp.concatenate([got[i:i + 1] for i in range(lines)], axis=1)

    def forward(g, sc):
        mine = dot(bt_ref[...], one_hots(ids(s_ref, g), rows), NN).astype(BF)
        own[:, span(g)] = mine
        rel = dot(rt[...], one_hots(ids(r_ref, g), rels), NN).astype(BF)
        rl[:, span(g)] = rel
        query = mine * rel
        qa[:, span(g)] = query
        sc[...] = dot(p[...], query, NN)
        hits = one_hots(n_ref[pl.ds(g, 1), :], rows)
        lanes = negs // 4
        four = (hits[:, :lanes] + hits[:, lanes:2 * lanes]) + (hits[:, 2 * lanes:3 * lanes] + hits[:, 3 * lanes:])
        times = jnp.sum(four.astype(F32), axis=1, keepdims=True) * (0.5 / negs)
        times_all[pl.ds(g, 1)] = jnp.broadcast_to(times, (rows, 128)).astype(BF)[None]

    def backward(g, sc):
        score = sc[...]
        row = lax.broadcasted_iota(jnp.int32, (rows, glen), 0)
        hit = row == ids(d_ref, g)
        positive = jnp.sum(jnp.where(hit, score, 0.0), axis=0, keepdims=True)
        pos_grad = 0.5 * jnp.tanh(positive) - 0.5
        times = times_all[pl.ds(g, 1)][0].astype(F32)
        times = jnp.concatenate([times, times], axis=1)
        weight = (jnp.tanh(score) + 1.0) * times
        weight = jnp.where(hit, weight + pos_grad, weight).astype(BF)
        wa[:, span(g)] = weight
        grad = dot(pt[...], weight, NN).astype(BF)
        xo_ref[:, span(g)] = grad * rl[:, span(g)]
        xr[:, span(g)] = grad * own[:, span(g)]

    forward(0, sc0)

    def pair(i, carry):
        forward(2 * i + 1, sc1)
        backward(2 * i, sc0)
        forward(jnp.minimum(2 * i + 2, groups - 1), sc0)
        backward(2 * i + 1, sc1)
        return carry

    lax.fori_loop(0, groups // 2, pair, 0)

    def onto_rows(t, carry):
        at = pl.ds(pl.multiple_of(t * TILE, TILE), TILE)
        part_ref[:, at] = dot(qa[...], wa[at, :], NT).astype(BF)
        return carry

    lax.fori_loop(0, rows // TILE, onto_rows, 0)
    tiles = half // TILE

    def scatter(t, carry):
        out = dot(xr[...], one_hot(rall_ref[...], t), NT).T.astype(BF)
        at = pl.ds(pl.multiple_of(lax.rem(t, tiles) * TILE, TILE), TILE)

        @pl.when(t < tiles)
        def _():
            g0_ref[at, :] = out

        @pl.when(t >= tiles)
        def _():
            g1_ref[at, :] = out

        return carry

    lax.fori_loop(0, rels // TILE, scatter, 0)


def last_kernel(xo_ref, sall_ref, own_ref):
    def onto_rows(t, carry):
        own_ref[:, pl.ds(pl.multiple_of(t * TILE, TILE), TILE)] = dot(xo_ref[...], one_hot(sall_ref[...], t), NT)
        return carry

    lax.fori_loop(0, own_ref.shape[1] // TILE, onto_rows, 0)


def swap(value, mask):
    pairs = [(source, source ^ mask) for source in range(lax.axis_size("dom"))]
    return lax.ppermute(value, "dom", pairs)


def groups_of(shift, bits):
    members = [m << shift for m in range(1 << bits)]
    rest = [b for b in range(lax.axis_size("dom")) if not b & (((1 << bits) - 1) << shift)]
    return [[b | m for m in members] for b in rest]


def exchange(blocks, shift, bits):
    return lax.all_to_all(blocks, "dom", 0, 0, axis_index_groups=groups_of(shift, bits))


def partner_step(mask, shift, bits, value):
    def branch(digit):
        return lambda moved: swap(moved, digit << shift) if digit else moved

    digit = jnp.bitwise_and(jnp.right_shift(mask, shift), (1 << bits) - 1)
    return lax.switch(digit, [branch(m) for m in range(1 << bits)], value)


def added(blocks):
    return jnp.sum(blocks.astype(F32), axis=0).astype(BF)


def local(
    embeddings,
    row_state,
    relations,
    relation_state,
    partner_mask,
    source_rows,
    relation_ids,
    dest_rows,
    negative_rows,
    edge_count,
):
    mask = partner_mask[0]
    groups = negative_rows.shape[0]
    rel_local, width = relations.shape
    rows = embeddings.shape[0]
    edges = source_rows.shape[0]
    me = lax.axis_index("dom")
    odd = jnp.bitwise_and(mask, 1) == 1
    z_size, xy_size = 1 << Z_BITS, 1 << XY_BITS
    half = z_size * xy_size * rel_local
    vm = pl.BlockSpec(memory_space=pltpu.VMEM)
    sh = jax.ShapeDtypeStruct

    own_t = embeddings.astype(BF).T
    rel_bf = relations.astype(BF)

    def spread(block, size):
        return jnp.broadcast_to(block[None], (size,) + block.shape)

    part_t = partner_step(mask, XY_SHIFT, XY_BITS, own_t)
    rel_z = exchange(spread(rel_bf, z_size), Z_SHIFT, Z_BITS).reshape(z_size * rel_local, width)
    rel_z, part_t = lax.optimization_barrier((rel_z, part_t))
    part_t = partner_step(mask, Z_SHIFT, Z_BITS, part_t)
    rel_here = exchange(spread(rel_z, xy_size), XY_SHIFT, XY_BITS)
    rel_here, part_t = lax.optimization_barrier((rel_here, part_t))
    rel_there = swap(rel_here, 1)
    part_there = swap(part_t, 1)

    owner = relation_ids // rel_local
    core = jnp.bitwise_and(jnp.bitwise_xor(owner, me), 1)
    spot = core * half + jnp.right_shift(owner, CORE_BITS) * rel_local + relation_ids % rel_local

    live_sources = jnp.where(jnp.arange(edges, dtype=jnp.int32) < edge_count[0], source_rows, -1)

    part_grad, to_source, grad_here, grad_there = pl.pallas_call(
        train_kernel,
        out_shape=(sh((width, rows), BF), sh((width, edges), BF), sh((half, width), BF), sh((half, width), BF)),
        in_specs=[pl.BlockSpec(memory_space=pltpu.SMEM)] + [vm] * 10, out_specs=(vm,) * 4,
        scratch_shapes=[pltpu.VMEM((width, 2 * half), BF), pltpu.VMEM((width, rows), BF), pltpu.VMEM((rows, width), BF),
                        *[pltpu.VMEM((width, edges), BF)] * 3, pltpu.VMEM((rows, edges), BF), pltpu.VMEM((width, edges), BF),
                        pltpu.VMEM((groups, rows, 128), BF),
                        pltpu.VMEM((rows, edges // groups), F32), pltpu.VMEM((rows, edges // groups), F32)],
        name="train",
    )(jnp.bitwise_and(partner_mask, 1), own_t, part_t, part_there,
      rel_here.reshape(half, width), rel_there.reshape(half, width),
      live_sources.reshape(-1, 128), spot.reshape(-1, 128), dest_rows.reshape(-1, 128), negative_rows,
      spot.reshape(1, edges))

    by_z = (xy_size, z_size * rel_local, width)
    from_core = swap(grad_there.reshape(by_z), 1)
    part_core = swap(part_grad, 1)
    own_grad = pl.pallas_call(
        last_kernel, out_shape=sh((width, rows), F32), in_specs=[vm] * 2, out_specs=vm, name="last",
    )(to_source, live_sources.reshape(1, edges))
    returned = jnp.where(odd, part_core, part_grad)
    grad_sum = (grad_here.reshape(by_z).astype(F32) + from_core.astype(F32)).astype(BF)
    grad_xy = added(exchange(grad_sum, XY_SHIFT, XY_BITS))
    returned = partner_step(mask, Z_SHIFT, Z_BITS, returned)
    grad_xy, returned, own_grad = lax.optimization_barrier((grad_xy, returned, own_grad))
    grad_z = exchange(grad_xy.reshape(z_size, rel_local, width), Z_SHIFT, Z_BITS)
    returned = partner_step(mask, XY_SHIFT, XY_BITS, returned)

    grad = (own_grad + returned.astype(F32)).T
    new_row_state = row_state + jnp.mean(grad * grad, axis=1)
    new_embeddings = embeddings - 0.1 * grad / jnp.sqrt(new_row_state)[:, None]
    rel_total = jnp.sum(grad_z.astype(F32), axis=0)
    new_relation_state = relation_state + jnp.mean(rel_total * rel_total, axis=1)
    new_relations = relations - 0.1 * rel_total / jnp.sqrt(new_relation_state)[:, None]
    return (new_embeddings, new_row_state, new_relations, new_relation_state)


def solution(mesh):
    in_specs = (
        P("dom", None),
        P("dom"),
        P("dom", None),
        P("dom"),
        P(),
        P("dom"),
        P("dom"),
        P("dom"),
        P("dom", None),
        P("dom"),
    )
    out_specs = (P("dom", None), P("dom"), P("dom", None), P("dom"))
    return jax.shard_map(local, mesh=mesh, in_specs=in_specs, out_specs=out_specs, check_vma=False)
```

```python
import jax
import jax.numpy as jnp
from jax import lax
from jax.experimental import pallas as pl
from jax.experimental.pallas import tpu as pltpu
from jax.sharding import PartitionSpec as P

BF = jnp.bfloat16
F32 = jnp.float32
NT = (((1,), (1,)), ((), ()))
NN = (((1,), (0,)), ((), ()))

CORE_BITS, Z_BITS, XY_BITS = 1, 3, 4
Z_SHIFT, XY_SHIFT = CORE_BITS, CORE_BITS + Z_BITS


TILE = 256
VL = 50


def dot(a, b, dims):
    return lax.dot_general(a, b, dims, preferred_element_type=F32)


def one_hot(ids, tile):
    low = jnp.where(jnp.right_shift(ids, 8) == tile, jnp.bitwise_and(ids, TILE - 1), -1)
    low = jnp.broadcast_to(low.astype(F32), (TILE, ids.shape[1])).astype(BF)
    rows = lax.broadcasted_iota(jnp.int32, (TILE, ids.shape[1]), 0).astype(F32).astype(BF)
    return jnp.where(rows == low, jnp.ones((), BF), jnp.zeros((), BF))


def one_hots(ids, size):
    return jnp.concatenate([one_hot(ids, t) for t in range(size // TILE)], axis=0)


def identity(n):
    return (lax.broadcasted_iota(jnp.int32, (n, n), 0) == lax.broadcasted_iota(jnp.int32, (n, n), 1)).astype(BF)


def line(values):
    return jnp.concatenate([values[i:i + 1] for i in range(values.shape[0])], axis=1)


def live_sources(count_ref, s_ref):
    lines, lanes = s_ref.shape
    edge = lax.broadcasted_iota(jnp.int32, (lines, lanes), 0) * lanes + lax.broadcasted_iota(jnp.int32, (lines, lanes), 1)
    return jnp.where(edge < count_ref[0], s_ref[...], -1)


def train_kernel(odd_ref, core_ref, count_ref, bt_in, pa_in, pb_in, r0_in, r1_in, sid_in, rid_in, d_in, n_in,
                 part_ref, xo_ref, g0_ref, g1_ref,
                 rt, pt, p, own, rl, qa, wa, xr, times_all, sc0, sc1, s_ref, r_ref, rall,
                 bt_ref, pa_ref, pb_ref, table, sid_ref, rid_ref, d_ref, n_ref, sems):
    half = r0_in.shape[0]
    moves = [
        pltpu.make_async_copy(source, target, sems.at[i])
        for i, (source, target) in enumerate((
            (pa_in, pa_ref), (pb_in, pb_ref), (sid_in, sid_ref), (rid_in, rid_ref),
            (r0_in, table.at[pl.ds(0, half)]), (r1_in, table.at[pl.ds(half, half)]),
            (bt_in, bt_ref), (n_in, n_ref), (d_in, d_ref)))
    ]
    for move in moves:
        move.start()
    width, rows = pa_ref.shape
    groups, negs = n_ref.shape
    edges = rall.shape[1]
    glen = edges // groups
    rels = 2 * half
    for move in moves[:4]:
        move.wait()
    s_ref[...] = live_sources(count_ref, sid_ref)
    rid = rid_ref[...]
    core = jnp.bitwise_and(jnp.bitwise_xor(jnp.right_shift(rid, 3), core_ref[0]), 1)
    spot = core * half + jnp.right_shift(rid, 4) * 8 + jnp.bitwise_and(rid, 7)
    r_ref[...] = spot
    rall[...] = line(spot)
    ident = identity(width)
    pt[...] = jnp.where(odd_ref[0] == 1, pb_ref[...], pa_ref[...])
    p[...] = (0.5 * pt[...].astype(F32)).T.astype(BF)
    for move in moves[4:]:
        move.wait()

    def turn(t, carry):
        at = pl.ds(pl.multiple_of(t * TILE, TILE), TILE)
        rt[:, at] = dot(ident, table[at, :], NT).astype(BF)
        return carry

    lax.fori_loop(0, rels // TILE, turn, 0)

    def span(g):
        return pl.ds(pl.multiple_of(g * glen, glen), glen)

    def ids(ref, g):
        return line(ref[pl.ds(g * (glen // 128), glen // 128), :])

    def forward(g, sc):
        mine = dot(bt_ref[...], one_hots(ids(s_ref, g), rows), NN).astype(BF)
        own[:, span(g)] = mine
        rel = dot(rt[...], one_hots(ids(r_ref, g), rels), NN).astype(BF)
        rl[:, span(g)] = rel
        query = mine * rel
        qa[:, span(g)] = query
        sc[...] = dot(p[...], query, NN)
        hits = one_hots(n_ref[pl.ds(g, 1), :], rows)
        lanes = negs // 4
        four = (hits[:, :lanes] + hits[:, lanes:2 * lanes]) + (hits[:, 2 * lanes:3 * lanes] + hits[:, 3 * lanes:])
        times = jnp.sum(four.astype(F32), axis=1, keepdims=True) * (0.5 / negs)
        times_all[pl.ds(g, 1)] = jnp.broadcast_to(times, (rows, 128)).astype(BF)[None]

    def backward(g, sc):
        score = sc[...]
        row = lax.broadcasted_iota(jnp.int32, (rows, glen), 0)
        hit = row == ids(d_ref, g)
        positive = jnp.sum(jnp.where(hit, score, 0.0), axis=0, keepdims=True)
        pos_grad = 0.5 * jnp.tanh(positive) - 0.5
        times = times_all[pl.ds(g, 1)][0].astype(F32)
        times = jnp.concatenate([times, times], axis=1)
        weight = (jnp.tanh(score) + 1.0) * times
        weight = jnp.where(hit, weight + pos_grad, weight).astype(BF)
        wa[:, span(g)] = weight
        grad = dot(pt[...], weight, NN).astype(BF)
        xo_ref[:, span(g)] = grad * rl[:, span(g)]
        xr[:, span(g)] = grad * own[:, span(g)]

    forward(0, sc0)

    def pair(i, carry):
        forward(2 * i + 1, sc1)
        backward(2 * i, sc0)
        forward(jnp.minimum(2 * i + 2, groups - 1), sc0)
        backward(2 * i + 1, sc1)
        return carry

    lax.fori_loop(0, groups // 2, pair, 0)

    def onto_rows(t, carry):
        at = pl.ds(pl.multiple_of(t * TILE, TILE), TILE)
        part_ref[:, at] = dot(qa[...], wa[at, :], NT).astype(BF)
        return carry

    lax.fori_loop(0, rows // TILE, onto_rows, 0)
    tiles = half // TILE

    def scatter(t, carry):
        out = dot(xr[...], one_hot(rall[...], t), NT).T.astype(BF)
        at = pl.ds(pl.multiple_of(lax.rem(t, tiles) * TILE, TILE), TILE)

        @pl.when(t < tiles)
        def _():
            g0_ref[at, :] = out

        @pl.when(t >= tiles)
        def _():
            g1_ref[at, :] = out

        return carry

    lax.fori_loop(0, rels // TILE, scatter, 0)


def last_kernel(count_ref, xo_ref, sid_ref, own_ref):
    sall = line(live_sources(count_ref, sid_ref))

    def onto_rows(t, carry):
        own_ref[:, pl.ds(pl.multiple_of(t * TILE, TILE), TILE)] = dot(xo_ref[...], one_hot(sall, t), NT)
        return carry

    lax.fori_loop(0, own_ref.shape[1] // TILE, onto_rows, 0)


def swap(value, mask):
    pairs = [(source, source ^ mask) for source in range(lax.axis_size("dom"))]
    return lax.ppermute(value, "dom", pairs)


def groups_of(shift, bits):
    members = [m << shift for m in range(1 << bits)]
    rest = [b for b in range(lax.axis_size("dom")) if not b & (((1 << bits) - 1) << shift)]
    return [[b | m for m in members] for b in rest]


def exchange(blocks, shift, bits):
    return lax.all_to_all(blocks, "dom", 0, 0, axis_index_groups=groups_of(shift, bits))


def partner_step(mask, shift, bits, value):
    def branch(digit):
        return lambda moved: swap(moved, digit << shift) if digit else moved

    digit = jnp.bitwise_and(jnp.right_shift(mask, shift), (1 << bits) - 1)
    return lax.switch(digit, [branch(m) for m in range(1 << bits)], value)


def added(blocks):
    return jnp.sum(blocks.astype(F32), axis=0).astype(BF)


def local(
    embeddings,
    row_state,
    relations,
    relation_state,
    partner_mask,
    source_rows,
    relation_ids,
    dest_rows,
    negative_rows,
    edge_count,
):
    mask = partner_mask[0]
    groups = negative_rows.shape[0]
    rel_local, width = relations.shape
    rows = embeddings.shape[0]
    edges = source_rows.shape[0]
    me = lax.axis_index("dom")
    odd = jnp.bitwise_and(mask, 1) == 1
    z_size, xy_size = 1 << Z_BITS, 1 << XY_BITS
    half = z_size * xy_size * rel_local
    vm = pl.BlockSpec(memory_space=pltpu.VMEM)
    sm = pl.BlockSpec(memory_space=pltpu.SMEM)
    sh = jax.ShapeDtypeStruct

    own_t = embeddings.astype(BF).T
    rel_bf = relations.astype(BF)

    def spread(block, size):
        return jnp.broadcast_to(block[None], (size,) + block.shape)

    part_t = partner_step(mask, XY_SHIFT, XY_BITS, own_t)
    rel_z = exchange(spread(rel_bf, z_size), Z_SHIFT, Z_BITS).reshape(z_size * rel_local, width)
    rel_z, part_t = lax.optimization_barrier((rel_z, part_t))
    part_t = partner_step(mask, Z_SHIFT, Z_BITS, part_t)
    rel_here = exchange(spread(rel_z, xy_size), XY_SHIFT, XY_BITS)
    rel_here, part_t = lax.optimization_barrier((rel_here, part_t))
    rel_there = swap(rel_here, 1)
    part_there = swap(part_t, 1)

    lines = (edges // 128, 128)
    part_grad, to_source, grad_here, grad_there = pl.pallas_call(
        train_kernel,
        out_shape=(sh((width, rows), BF), sh((width, edges), BF), sh((half, width), BF), sh((half, width), BF)),
        in_specs=[sm] * 3 + [pl.BlockSpec(memory_space=pltpu.HBM)] * 9, out_specs=(vm,) * 4,
        scratch_shapes=[pltpu.VMEM((width, 2 * half), BF), pltpu.VMEM((width, rows), BF), pltpu.VMEM((rows, width), BF),
                        *[pltpu.VMEM((width, edges), BF)] * 3, pltpu.VMEM((rows, edges), BF), pltpu.VMEM((width, edges), BF),
                        pltpu.VMEM((groups, rows, 128), BF), pltpu.VMEM((rows, edges // groups), F32),
                        pltpu.VMEM((rows, edges // groups), F32), pltpu.VMEM(lines, jnp.int32),
                        pltpu.VMEM(lines, jnp.int32), pltpu.VMEM((1, edges), jnp.int32),
                        *[pltpu.VMEM((width, rows), BF)] * 3, pltpu.VMEM((2 * half, width), BF),
                        *[pltpu.VMEM(lines, jnp.int32)] * 3, pltpu.VMEM(negative_rows.shape, jnp.int32),
                        pltpu.SemaphoreType.DMA((9,))],
        compiler_params=pltpu.CompilerParams(vmem_limit_bytes=VL << 20),
        name="train",
    )(jnp.bitwise_and(partner_mask, 1), jnp.bitwise_and(me, 1).reshape(1), edge_count, own_t, part_t, part_there,
      rel_here.reshape(half, width), rel_there.reshape(half, width),
      source_rows.reshape(lines), relation_ids.reshape(lines), dest_rows.reshape(lines), negative_rows)

    by_z = (xy_size, z_size * rel_local, width)
    from_core = swap(grad_there.reshape(by_z), 1)
    part_core = swap(part_grad, 1)
    own_grad = pl.pallas_call(
        last_kernel, out_shape=sh((width, rows), F32), in_specs=[sm] + [vm] * 2, out_specs=vm, name="last",
        compiler_params=pltpu.CompilerParams(vmem_limit_bytes=16 << 20),
    )(edge_count, to_source, source_rows.reshape(lines))
    returned = jnp.where(odd, part_core, part_grad)
    grad_sum = (grad_here.reshape(by_z).astype(F32) + from_core.astype(F32)).astype(BF)
    grad_xy = added(exchange(grad_sum, XY_SHIFT, XY_BITS))
    returned = partner_step(mask, Z_SHIFT, Z_BITS, returned)
    grad_xy, returned, own_grad = lax.optimization_barrier((grad_xy, returned, own_grad))
    grad_z = exchange(grad_xy.reshape(z_size, rel_local, width), Z_SHIFT, Z_BITS)
    returned = partner_step(mask, XY_SHIFT, XY_BITS, returned)

    grad = (own_grad + returned.astype(F32)).T
    new_row_state = row_state + jnp.mean(grad * grad, axis=1)
    new_embeddings = embeddings - 0.1 * grad / jnp.sqrt(new_row_state)[:, None]
    rel_total = jnp.sum(grad_z.astype(F32), axis=0)
    new_relation_state = relation_state + jnp.mean(rel_total * rel_total, axis=1)
    new_relations = relations - 0.1 * rel_total / jnp.sqrt(new_relation_state)[:, None]
    return (new_embeddings, new_row_state, new_relations, new_relation_state)


def solution(mesh):
    in_specs = (
        P("dom", None),
        P("dom"),
        P("dom", None),
        P("dom"),
        P(),
        P("dom"),
        P("dom"),
        P("dom"),
        P("dom", None),
        P("dom"),
    )
    out_specs = (P("dom", None), P("dom"), P("dom", None), P("dom"))
    return jax.shard_map(local, mesh=mesh, in_specs=in_specs, out_specs=out_specs, check_vma=False)
```

```python
import jax
import jax.numpy as jnp
from jax import lax
from jax.experimental import pallas as pl
from jax.experimental.pallas import tpu as pltpu
from jax.sharding import PartitionSpec as P

BF = jnp.bfloat16
F32 = jnp.float32
NT = (((1,), (1,)), ((), ()))
NN = (((1,), (0,)), ((), ()))

CORE_BITS, Z_BITS, XY_BITS = 1, 3, 4
Z_SHIFT, XY_SHIFT = CORE_BITS, CORE_BITS + Z_BITS


TILE = 256
VL = 50


def dot(a, b, dims):
    return lax.dot_general(a, b, dims, preferred_element_type=F32)


def one_hot(ids, tile):
    low = jnp.where(jnp.right_shift(ids, 8) == tile, jnp.bitwise_and(ids, TILE - 1), -1)
    low = jnp.broadcast_to(low.astype(F32), (TILE, ids.shape[1])).astype(BF)
    rows = lax.broadcasted_iota(jnp.int32, (TILE, ids.shape[1]), 0).astype(F32).astype(BF)
    return jnp.where(rows == low, jnp.ones((), BF), jnp.zeros((), BF))


def one_hots(ids, size):
    return jnp.concatenate([one_hot(ids, t) for t in range(size // TILE)], axis=0)


def identity(n):
    return (lax.broadcasted_iota(jnp.int32, (n, n), 0) == lax.broadcasted_iota(jnp.int32, (n, n), 1)).astype(BF)


def line(values):
    return jnp.concatenate([values[i:i + 1] for i in range(values.shape[0])], axis=1)


def live_sources(count_ref, s_ref):
    lines, lanes = s_ref.shape
    edge = lax.broadcasted_iota(jnp.int32, (lines, lanes), 0) * lanes + lax.broadcasted_iota(jnp.int32, (lines, lanes), 1)
    return jnp.where(edge < count_ref[0], s_ref[...], -1)


def train_kernel(odd_ref, core_ref, count_ref, bt_in, pa_in, pb_in, r0_in, r1_in, sid_in, rid_in, d_in, n_in,
                 part_ref, xo_ref, g0_ref, g1_ref,
                 rt, pt, p, own, rl, qa, wa, xr, times_all, sc0, sc1, s_ref, r_ref, rall,
                 bt_ref, pa_ref, pb_ref, table, sid_ref, rid_ref, d_ref, n_ref, sems):
    half = r0_in.shape[0]
    moves = [
        pltpu.make_async_copy(source, target, sems.at[i])
        for i, (source, target) in enumerate((
            (pa_in, pa_ref), (pb_in, pb_ref), (sid_in, sid_ref), (rid_in, rid_ref),
            (r0_in, table.at[pl.ds(0, half)]), (r1_in, table.at[pl.ds(half, half)]),
            (bt_in, bt_ref), (n_in, n_ref), (d_in, d_ref)))
    ]
    for move in moves:
        move.start()
    width, rows = pa_ref.shape
    groups, negs = n_ref.shape
    edges = rall.shape[1]
    glen = edges // groups
    rels = 2 * half
    for move in moves[:4]:
        move.wait()
    s_ref[...] = live_sources(count_ref, sid_ref)
    rid = rid_ref[...]
    core = jnp.bitwise_and(jnp.bitwise_xor(jnp.right_shift(rid, 3), core_ref[0]), 1)
    spot = core * half + jnp.right_shift(rid, 4) * 8 + jnp.bitwise_and(rid, 7)
    r_ref[...] = spot
    rall[...] = line(spot)
    ident = identity(width)
    pt[...] = jnp.where(odd_ref[0] == 1, pb_ref[...], pa_ref[...])
    p[...] = (0.5 * pt[...].astype(F32)).T.astype(BF)
    for move in moves[4:]:
        move.wait()

    def turn(t, carry):
        at = pl.ds(pl.multiple_of(t * TILE, TILE), TILE)
        rt[:, at] = dot(ident, table[at, :], NT).astype(BF)
        return carry

    lax.fori_loop(0, rels // TILE, turn, 0)

    def span(g):
        return pl.ds(pl.multiple_of(g * glen, glen), glen)

    def ids(ref, g):
        return line(ref[pl.ds(g * (glen // 128), glen // 128), :])

    def forward(g, sc):
        mine = dot(bt_ref[...], one_hots(ids(s_ref, g), rows), NN).astype(BF)
        own[:, span(g)] = mine
        rel = dot(rt[...], one_hots(ids(r_ref, g), rels), NN).astype(BF)
        rl[:, span(g)] = rel
        query = mine * rel
        qa[:, span(g)] = query
        sc[...] = dot(p[...], query, NN)
        hits = one_hots(n_ref[pl.ds(g, 1), :], rows)
        lanes = negs // 4
        four = (hits[:, :lanes] + hits[:, lanes:2 * lanes]) + (hits[:, 2 * lanes:3 * lanes] + hits[:, 3 * lanes:])
        times = jnp.sum(four.astype(F32), axis=1, keepdims=True) * (0.5 / negs)
        times_all[pl.ds(g, 1)] = jnp.broadcast_to(times, (rows, 128)).astype(BF)[None]

    def backward(g, sc):
        score = sc[...]
        row = lax.broadcasted_iota(jnp.int32, (rows, glen), 0)
        hit = row == ids(d_ref, g)
        positive = jnp.sum(jnp.where(hit, score, 0.0), axis=0, keepdims=True)
        pos_grad = 0.5 * jnp.tanh(positive) - 0.5
        times = times_all[pl.ds(g, 1)][0].astype(F32)
        times = jnp.concatenate([times, times], axis=1)
        weight = (jnp.tanh(sc[...]) + 1.0) * times
        again = (row + rows) == (ids(d_ref, g) + rows)
        weight = (weight + jnp.where(again, pos_grad, 0.0)).astype(BF)
        wa[:, span(g)] = weight
        grad = dot(pt[...], weight, NN).astype(BF)
        xo_ref[:, span(g)] = grad * rl[:, span(g)]
        xr[:, span(g)] = grad * own[:, span(g)]

    forward(0, sc0)

    def pair(i, carry):
        forward(2 * i + 1, sc1)
        backward(2 * i, sc0)
        forward(jnp.minimum(2 * i + 2, groups - 1), sc0)
        backward(2 * i + 1, sc1)
        return carry

    lax.fori_loop(0, groups // 2, pair, 0)

    def onto_rows(t, carry):
        at = pl.ds(pl.multiple_of(t * TILE, TILE), TILE)
        part_ref[:, at] = dot(qa[...], wa[at, :], NT).astype(BF)
        return carry

    lax.fori_loop(0, rows // TILE, onto_rows, 0)
    tiles = half // TILE

    def scatter(t, carry):
        out = dot(xr[...], one_hot(rall[...], t), NT).T.astype(BF)
        at = pl.ds(pl.multiple_of(lax.rem(t, tiles) * TILE, TILE), TILE)

        @pl.when(t < tiles)
        def _():
            g0_ref[at, :] = out

        @pl.when(t >= tiles)
        def _():
            g1_ref[at, :] = out

        return carry

    lax.fori_loop(0, rels // TILE, scatter, 0)


def last_kernel(count_ref, xo_ref, sid_ref, own_ref):
    sall = line(live_sources(count_ref, sid_ref))

    def onto_rows(t, carry):
        own_ref[:, pl.ds(pl.multiple_of(t * TILE, TILE), TILE)] = dot(xo_ref[...], one_hot(sall, t), NT)
        return carry

    lax.fori_loop(0, own_ref.shape[1] // TILE, onto_rows, 0)


def swap(value, mask):
    pairs = [(source, source ^ mask) for source in range(lax.axis_size("dom"))]
    return lax.ppermute(value, "dom", pairs)


def groups_of(shift, bits):
    members = [m << shift for m in range(1 << bits)]
    rest = [b for b in range(lax.axis_size("dom")) if not b & (((1 << bits) - 1) << shift)]
    return [[b | m for m in members] for b in rest]


def exchange(blocks, shift, bits):
    return lax.all_to_all(blocks, "dom", 0, 0, axis_index_groups=groups_of(shift, bits))


def partner_step(mask, shift, bits, value):
    def branch(digit):
        return lambda moved: swap(moved, digit << shift) if digit else moved

    digit = jnp.bitwise_and(jnp.right_shift(mask, shift), (1 << bits) - 1)
    return lax.switch(digit, [branch(m) for m in range(1 << bits)], value)


def added(blocks):
    return jnp.sum(blocks.astype(F32), axis=0).astype(BF)


def local(
    embeddings,
    row_state,
    relations,
    relation_state,
    partner_mask,
    source_rows,
    relation_ids,
    dest_rows,
    negative_rows,
    edge_count,
):
    mask = partner_mask[0]
    groups = negative_rows.shape[0]
    rel_local, width = relations.shape
    rows = embeddings.shape[0]
    edges = source_rows.shape[0]
    me = lax.axis_index("dom")
    odd = jnp.bitwise_and(mask, 1) == 1
    z_size, xy_size = 1 << Z_BITS, 1 << XY_BITS
    half = z_size * xy_size * rel_local
    vm = pl.BlockSpec(memory_space=pltpu.VMEM)
    sm = pl.BlockSpec(memory_space=pltpu.SMEM)
    sh = jax.ShapeDtypeStruct

    own_t = embeddings.astype(BF).T
    rel_bf = relations.astype(BF)

    def spread(block, size):
        return jnp.broadcast_to(block[None], (size,) + block.shape)

    part_t = partner_step(mask, XY_SHIFT, XY_BITS, own_t)
    rel_z = exchange(spread(rel_bf, z_size), Z_SHIFT, Z_BITS).reshape(z_size * rel_local, width)
    rel_z, part_t = lax.optimization_barrier((rel_z, part_t))
    part_t = partner_step(mask, Z_SHIFT, Z_BITS, part_t)
    rel_here = exchange(spread(rel_z, xy_size), XY_SHIFT, XY_BITS)
    rel_here, part_t = lax.optimization_barrier((rel_here, part_t))
    rel_there = swap(rel_here, 1)
    part_there = swap(part_t, 1)

    lines = (edges // 128, 128)
    part_grad, to_source, grad_here, grad_there = pl.pallas_call(
        train_kernel,
        out_shape=(sh((width, rows), BF), sh((width, edges), BF), sh((half, width), BF), sh((half, width), BF)),
        in_specs=[sm] * 3 + [pl.BlockSpec(memory_space=pltpu.HBM)] * 9, out_specs=(vm,) * 4,
        scratch_shapes=[pltpu.VMEM((width, 2 * half), BF), pltpu.VMEM((width, rows), BF), pltpu.VMEM((rows, width), BF),
                        *[pltpu.VMEM((width, edges), BF)] * 3, pltpu.VMEM((rows, edges), BF), pltpu.VMEM((width, edges), BF),
                        pltpu.VMEM((groups, rows, 128), BF), pltpu.VMEM((rows, edges // groups), F32),
                        pltpu.VMEM((rows, edges // groups), F32), pltpu.VMEM(lines, jnp.int32),
                        pltpu.VMEM(lines, jnp.int32), pltpu.VMEM((1, edges), jnp.int32),
                        *[pltpu.VMEM((width, rows), BF)] * 3, pltpu.VMEM((2 * half, width), BF),
                        *[pltpu.VMEM(lines, jnp.int32)] * 3, pltpu.VMEM(negative_rows.shape, jnp.int32),
                        pltpu.SemaphoreType.DMA((9,))],
        compiler_params=pltpu.CompilerParams(
            vmem_limit_bytes=VL << 20),
        name="train",
    )(jnp.bitwise_and(partner_mask, 1), jnp.bitwise_and(me, 1).reshape(1), edge_count, own_t, part_t, part_there,
      rel_here.reshape(half, width), rel_there.reshape(half, width),
      source_rows.reshape(lines), relation_ids.reshape(lines), dest_rows.reshape(lines), negative_rows)

    by_z = (xy_size, z_size * rel_local, width)
    from_core = swap(grad_there.reshape(by_z), 1)
    part_core = swap(part_grad, 1)
    own_grad = pl.pallas_call(
        last_kernel, out_shape=sh((width, rows), F32), in_specs=[sm] + [vm] * 2, out_specs=vm, name="last",
        compiler_params=pltpu.CompilerParams(vmem_limit_bytes=58 << 20),
    )(edge_count, to_source, source_rows.reshape(lines))
    returned = jnp.where(odd, part_core, part_grad)
    grad_sum = (grad_here.reshape(by_z).astype(F32) + from_core.astype(F32)).astype(BF)
    grad_xy = added(exchange(grad_sum, XY_SHIFT, XY_BITS))
    returned = partner_step(mask, Z_SHIFT, Z_BITS, returned)
    grad_xy, returned, own_grad = lax.optimization_barrier((grad_xy, returned, own_grad))
    grad_z = exchange(grad_xy.reshape(z_size, rel_local, width), Z_SHIFT, Z_BITS)
    returned = partner_step(mask, XY_SHIFT, XY_BITS, returned)

    grad = (own_grad + returned.astype(F32)).T
    new_row_state = row_state + jnp.mean(grad * grad, axis=1)
    new_embeddings = embeddings - 0.1 * grad / jnp.sqrt(new_row_state)[:, None]
    rel_total = jnp.sum(grad_z.astype(F32), axis=0)
    new_relation_state = relation_state + jnp.mean(rel_total * rel_total, axis=1)
    new_relations = relations - 0.1 * rel_total / jnp.sqrt(new_relation_state)[:, None]
    return (new_embeddings, new_row_state, new_relations, new_relation_state)


def solution(mesh):
    in_specs = (
        P("dom", None),
        P("dom"),
        P("dom", None),
        P("dom"),
        P(),
        P("dom"),
        P("dom"),
        P("dom"),
        P("dom", None),
        P("dom"),
    )
    out_specs = (P("dom", None), P("dom"), P("dom", None), P("dom"))
    return jax.shard_map(local, mesh=mesh, in_specs=in_specs, out_specs=out_specs, check_vma=False)
```
